32 devices in a mesh: dp: 8 (over z, x), expert: 4 (over y, core).
Axes of the slice: x: 2, y: 2, z: 4, core: 2. Of those that a mesh axis runs over, the one named last changes fastest.
Arguments:
- inputs: bfloat16 [32, 128, 2048], P(('dp', 'expert')), may hold values from -6 to 6
- cotangent: bfloat16 [32, 128, 2048], P(('dp', 'expert')), may hold values from -6 to 6
- lengths: int32 [32], P('dp'), may hold values from 1 to 128, 3072 in all
- dealing: int32 [8, 4], P('dp'), may hold values from 0 to 3, each once within a row
- routes: int32 [32, 128, 8], P(('dp', 'expert')), may hold values from 0 to 15, all different within a row; in each aligned block of 128 rows (0 to 127, 128 to 255, ..., all dimensions but the last counted through in order) at most 72 rows name the same one
- gate_values: float32 [32, 128, 8], P(('dp', 'expert')), may hold values from 0.25 to 0.75
- attn_gain: float32 [2048], replicated, may hold values from 0.1 to 1.9
- w_query: float32 [2048, 2048], P(('dp', 'expert')), may hold values from -0.125 to 0.125
- w_key: float32 [2048, 2048], P(('dp', 'expert')), may hold values from -0.125 to 0.125
- w_value: float32 [2048, 2048], P(('dp', 'expert')), may hold values from -0.125 to 0.125
- query_gain: float32 [2048], replicated, may hold values from 0.1 to 1.9
- key_gain: float32 [2048], replicated, may hold values from 0.1 to 1.9
- w_out: float32 [2048, 2048], P(('dp', 'expert')), may hold values from -0.5 to 0.5
- ffn_gain: float32 [2048], replicated, may hold values from 0.1 to 1.9
- w_gate: float32 [16, 2048, 1024], P('expert', 'dp'), may hold values from -0.125 to 0.125
- w_up: float32 [16, 2048, 1024], P('expert', 'dp'), may hold values from -0.125 to 0.125
- w_down: float32 [16, 1024, 2048], P('expert', 'dp'), may hold values from -0.1875 to 0.1875
Outputs:
- layer_out: bfloat16 [32, 128, 2048], P(('dp', 'expert'))
- grad_inputs: bfloat16 [32, 128, 2048], P(('dp', 'expert'))
- grad_attn_gain: float32 [2048], P(('dp', 'expert'))
- grad_w_query: float32 [2048, 2048], P(('dp', 'expert'))
- grad_w_key: float32 [2048, 2048], P(('dp', 'expert'))
- grad_w_value: float32 [2048, 2048], P(('dp', 'expert'))
- grad_query_gain: float32 [2048], P(('dp', 'expert'))
- grad_key_gain: float32 [2048], P(('dp', 'expert'))
- grad_w_out: float32 [2048, 2048], P(('dp', 'expert'))
- grad_ffn_gain: float32 [2048], P(('dp', 'expert'))
- grad_w_gate: float32 [16, 2048, 1024], P('expert', 'dp')
- grad_w_up: float32 [16, 2048, 1024], P('expert', 'dp')
- grad_w_down: float32 [16, 1024, 2048], P('expert', 'dp')
The draws below stay inside these ranges and needn't reach their ends.
Inputs may be any that keep to these rules, and one draw needn't show every extreme that they name: `lengths`: the longest sequence has exactly 128 tokens. `dealing`: each row names every sequence of its group once. `routes`: each token names 8 different experts; within one dealt sequence no expert is named more than 72 times, and some sequence reaches 72 in every draw.
All inputs are finite; a program needn't handle non-finite values. No bound on the sum of `lengths` on one device may be relied on, other than what follows from the above.
Results may differ from the reference program's by a relative error of at most 0.015.
Values may be sent and summed in bfloat16 or wider, within the bound.
A program may use at most 384 MiB of HBM per device.

```python
import math
import jax
import jax.numpy as jnp
import numpy as np
from jax import lax

D = 2048
HEADS = 16
FF = 1024
TOP = 8
LEN = 128
GROUP = 4
SEQS = 32
EXPERTS = 16
CAP = 72
N_DP = 8


def shard_levels(stream_key, dims, cuts, least, high):
    def one(dim, blocks):
        heights = jax.random.uniform(jax.random.fold_in(jax.random.fold_in(stream_key, 6), dim), (blocks,), jnp.float32, least / len(cuts), high / len(cuts))
        return jnp.repeat(jnp.exp(heights), dims[dim] // blocks).reshape((-1,) + (1,) * (len(dims) - dim - 1))

    factor_of = one(*cuts[0])
    for cut in cuts[1:]:
        factor_of = factor_of * one(*cut)
    return factor_of


def profile(count, total, reach, slope):
    portions = [(1 << 20) // math.isqrt(grade ** slope) + 1 for grade in range(2, count + 1)]
    rest, counts = total - reach - (count - 1), [1] * (count - 1)
    while rest > 0:
        movable = [i for i in range(count - 1) if counts[i] < reach]
        whole, budget = sum([portions[i] for i in movable]), rest
        for i in movable:
            more = min(reach - counts[i], max(1, budget * portions[i] // whole), rest)
            counts[i] = counts[i] + more
            rest = rest - more
    return np.array([reach] + counts)


def uneven(rng, amount, total, bound, skew):
    if amount == 2:
        one = jax.random.randint(rng, (), max(1, total - bound), min(bound, total - 1) + 1)
        return jnp.stack([one, total - one])
    tallies = jnp.asarray(profile(amount, total, bound, skew), jnp.int32)
    pairs = (amount - 1) // 2
    giver, taker = tallies[1:1 + 2 * pairs:2], tallies[2:2 + 2 * pairs:2]
    slack = jnp.minimum(giver - 1, bound - taker)
    moved = jax.random.randint(jax.random.fold_in(rng, 1), (pairs,), 0, 1 << 20) % (slack + 1)
    tallies = tallies.at[1:1 + 2 * pairs:2].set(giver - moved).at[2:2 + 2 * pairs:2].set(taker + moved)
    return tallies[jax.random.permutation(jax.random.fold_in(rng, 2), amount)]


def routed_block(stream_key, own, number, rows, count, top, limit, skew):
    sequence = jax.random.permutation(stream_key, count)
    crowded, usual = load_shares(count, rows * top, limit, skew, True), load_shares(count, rows * top, limit, skew, False)
    places = jnp.arange(count)

    def named(sizes, offset_by):
        used = int((sizes > 0).sum())
        fixed = max(1, used // 4)
        passed = fixed + (places - fixed + offset_by * (used - fixed)) % max(1, count - fixed)
        return jnp.zeros((count,), jnp.int32).at[sequence[jnp.where(places < fixed, places, passed)]].set(jnp.asarray(sizes, jnp.int32))

    sizes = jnp.where(number % 4 == 0, named(crowded, number // 4), named(usual, number - number // 4 - 1))
    mixed = jax.random.permutation(jax.random.fold_in(own, 3), count)
    donor, sink = mixed[0:count // 2 * 2:2], mixed[1:count // 2 * 2:2]
    room = jnp.minimum(sizes[donor] - 1, limit - sizes[sink]) // 2
    room = jnp.where((donor == sequence[0]) | (sink == sequence[0]) | (sizes[sink] == 0), 0, jnp.maximum(room, 0))
    passed = jax.random.randint(jax.random.fold_in(own, 4), (count // 2,), 0, 1 << 20) % (room + 1)
    sizes = sizes.at[donor].add(-passed).at[sink].add(passed)
    members = jnp.searchsorted(jnp.cumsum(sizes), jnp.arange(rows * top), side="right").astype(jnp.int32)
    listing = members.reshape(top, rows).T
    listing = listing[jax.random.permutation(jax.random.fold_in(own, 1), rows)]
    offset_by = jax.random.randint(jax.random.fold_in(own, 2), (rows, 1), 0, top)
    return jnp.take_along_axis(listing, (jnp.arange(top)[None, :] + offset_by) % top, axis=1)


def load_shares(amount, total, reach, lean, full):
    loads = [(1 << 20) // math.isqrt(rank ** lean) + 1 for rank in range(1, amount + 1)]
    largest = reach if full else min(reach, max(-(-total // amount), total * loads[0] // sum(loads)))
    least = 1 if total - largest >= amount - 1 else 0
    given, spare = [largest] + [least] * (amount - 1), total - largest - least * (amount - 1)
    while spare > 0:
        free = [i for i in range(1, amount) if given[i] < largest] or [i for i in range(1, amount) if given[i] < reach]
        whole, remaining = sum([loads[i] for i in free]), spare
        for i in free:
            extra = min(reach - given[i], max(1, remaining * loads[i] // whole), spare)
            given[i] = given[i] + extra
            spare = spare - extra
    return np.array(given)


def noise(rng, extent, spread, reach, pieces=(), kind=jnp.bfloat16):
    result = jax.random.normal(rng, extent, jnp.float32) * spread
    if len(pieces) > 0:
        result = shard_levels(rng, extent, pieces, -0.22, 0.18) * result
    return jnp.clip(result, min=-reach, max=reach).astype(kind)


def setup_inputs(seed: int = 0) -> dict:
    key_list = jax.random.split(jax.random.key(seed), 18)
    inputs = noise(key_list[0], (SEQS, LEN, D), 1.0, 6.0, ((0, 32),))
    cotangent = noise(key_list[1], (SEQS, LEN, D), 1.0, 6.0, ((0, 32),))
    lengths = uneven(key_list[2], SEQS, SEQS * LEN * 3 // 4, LEN, 1).astype(jnp.int32)
    dealing = jax.vmap(lambda own: jax.random.permutation(own, GROUP))(jax.random.split(key_list[3], N_DP)).reshape((N_DP, GROUP)).astype(jnp.int32)
    routes_keys = jax.random.split(jax.random.fold_in(key_list[4], 1), SEQS * LEN // LEN)
    routes_turns = jax.random.permutation(jax.random.fold_in(key_list[4], 3), SEQS * LEN // LEN)
    routes = jax.vmap(lambda own, number: routed_block(jax.random.fold_in(key_list[4], 2), own, number, LEN, EXPERTS, TOP, CAP, 1))(routes_keys, routes_turns).reshape((SEQS, LEN, TOP))
    gate_values = jnp.clip(0.25 + 0.5 * jax.random.uniform(key_list[5], (SEQS, LEN, TOP), jnp.float32) ** shard_levels(key_list[5], (SEQS, LEN, TOP), ((0, 32),), -0.2, 0.2), 0.25, 0.75)
    attn_gain = jnp.clip(1.0 + 0.18 * jax.random.normal(key_list[6], (D,), jnp.float32), 0.1, 1.9)
    w_query = noise(key_list[7], (D, D), D ** -0.5, 0.125, ((0, 32),), jnp.float32)
    w_key = noise(key_list[8], (D, D), D ** -0.5, 0.125, ((0, 32),), jnp.float32)
    w_value = noise(key_list[9], (D, D), D ** -0.5, 0.125, ((0, 32),), jnp.float32)
    query_gain = jnp.clip(1.0 + 0.18 * jax.random.normal(key_list[10], (D,), jnp.float32), 0.1, 1.9)
    key_gain = jnp.clip(1.0 + 0.18 * jax.random.normal(key_list[11], (D,), jnp.float32), 0.1, 1.9)
    w_out = noise(key_list[12], (D, D), (D // 16) ** -0.5, 0.5, ((0, 32),), jnp.float32)
    ffn_gain = jnp.clip(1.0 + 0.18 * jax.random.normal(key_list[13], (D,), jnp.float32), 0.1, 1.9)
    w_gate = noise(key_list[14], (EXPERTS, D, FF), D ** -0.5, 0.125, ((0, 4), (1, 8)), jnp.float32)
    w_up = noise(key_list[15], (EXPERTS, D, FF), D ** -0.5, 0.125, ((0, 4), (1, 8)), jnp.float32)
    w_down = noise(key_list[16], (EXPERTS, FF, D), FF ** -0.5, 0.1875, ((0, 4), (1, 8)), jnp.float32)
    return dict(inputs=inputs, cotangent=cotangent, lengths=lengths, dealing=dealing, routes=routes, gate_values=gate_values, attn_gain=attn_gain, w_query=w_query, w_key=w_key, w_value=w_value, query_gain=query_gain, key_gain=key_gain, w_out=w_out, ffn_gain=ffn_gain, w_gate=w_gate, w_up=w_up, w_down=w_down)


epsilon = 1e-05
highest = lax.Precision.HIGHEST

@jax.custom_vjp
def low(v):
    return lax.optimization_barrier(v.astype(jnp.bfloat16)).astype(jnp.float32)

@jax.custom_vjp
def low_back(v):
    return v

def low_keep(v):
    return (low(v), None)

def low_pass(kept, grad):
    return (grad,)

def back_keep(v):
    return (v, None)

def back_low(kept, grad):
    return (low(grad),)
low.defvjp(low_keep, low_pass)
low_back.defvjp(back_keep, back_low)

def norm_rows(values, gain):
    return values * lax.rsqrt(lax.optimization_barrier(jnp.mean(values * values, axis=-1, keepdims=True)) + epsilon) * gain

def angle_tables(length_rows, head_size):
    half_size = head_size // 2
    position = jnp.arange(length_rows, dtype=jnp.float32)[:, None]
    inverse = jnp.exp(jnp.arange(half_size, dtype=jnp.float32) * (-2.0 * math.log(10000.0) / head_size))
    angles = position * inverse[None, :]
    return (jnp.cos(angles)[:, None, :], jnp.sin(angles)[:, None, :])

def rotate_pairs(values, cosine, sine_table):
    half_size = values.shape[-1] // 2
    first = values[..., :half_size]
    second = values[..., half_size:]
    return jnp.concatenate([first * cosine - second * sine_table, second * cosine + first * sine_table], axis=-1)

def route_tables(expert_picks):
    flat_picks = expert_picks.reshape(-1)
    onehot = (flat_picks[:, None] == jnp.arange(EXPERTS, dtype=jnp.int32)[None, :]).astype(jnp.int32)
    before = jnp.cumsum(onehot, axis=0) - onehot
    rank_within = lax.optimization_barrier(jnp.sum(before * onehot, axis=1))
    slot_place = flat_picks * CAP + rank_within
    pair_count = flat_picks.shape[0]
    owner_pair = jnp.zeros((EXPERTS * CAP,), jnp.int32).at[slot_place].set(jnp.arange(pair_count, dtype=jnp.int32))
    filled = jnp.zeros((EXPERTS * CAP,), jnp.int32).at[slot_place].set(1)
    return (slot_place, owner_pair, filled)

def slot_layer(carried, params):
    seq_inputs, seq_length, expert_picks, gate_rows = carried
    attn_gain, w_query, w_key, w_value, query_gain, key_gain, w_out, ffn_gain, w_gate, w_up, w_down = params
    head_size = D // HEADS
    hidden_in = low(norm_rows(seq_inputs, attn_gain))
    query_raw = low_back(jnp.dot(hidden_in, w_query, precision=highest))
    key_raw = low_back(jnp.dot(hidden_in, w_key, precision=highest))
    values = low(low_back(jnp.dot(hidden_in, w_value, precision=highest)))
    cosine, sine_table = angle_tables(LEN, head_size)
    queries = low(rotate_pairs(norm_rows(query_raw, query_gain).reshape(LEN, HEADS, head_size), cosine, sine_table))
    key_rows = low(rotate_pairs(norm_rows(key_raw, key_gain).reshape(LEN, HEADS, head_size), cosine, sine_table))
    scores = low_back(jnp.einsum('ihd,jhd->hij', queries, key_rows, precision=highest) * head_size ** (-0.5))
    row_index = jnp.arange(LEN, dtype=jnp.int32)[:, None]
    col_index = jnp.arange(LEN, dtype=jnp.int32)[None, :]
    visible = (col_index <= row_index) & (col_index < seq_length)
    scores = jnp.where(visible[None], scores, -1e+30)
    weights = low(jax.nn.softmax(scores, axis=-1))
    attended = jnp.einsum('hij,jhd->ihd', weights, values.reshape(LEN, HEADS, head_size), precision=highest)
    attended = low(low_back(attended.reshape(LEN, D)))
    residual = seq_inputs + low_back(jnp.dot(attended, w_out, precision=highest))
    hidden_mid = low(norm_rows(residual, ffn_gain))
    slot_place, owner_pair, filled = route_tables(expert_picks)
    token_of_slot = owner_pair // TOP
    rows = low_back(hidden_mid[token_of_slot] * filled[:, None].astype(jnp.float32)).reshape(EXPERTS, CAP, D)
    gate_pre = low_back(jnp.einsum('ecd,edf->ecf', rows, w_gate, precision=highest))
    up_pre = low_back(jnp.einsum('ecd,edf->ecf', rows, w_up, precision=highest))
    hidden_act = low(jax.nn.silu(gate_pre) * up_pre)
    expert_out = low(low_back(jnp.einsum('ecf,efd->ecd', hidden_act, w_down, precision=highest))).reshape(EXPERTS * CAP, D)
    picked = expert_out[slot_place].reshape(LEN, TOP, D)
    return residual + lax.optimization_barrier(jnp.sum(gate_rows[:, :, None] * picked, axis=1))

def reference(inputs, cotangent, lengths, dealing, routes, gate_values, attn_gain, w_query, w_key, w_value, query_gain, key_gain, w_out, ffn_gain, w_gate, w_up, w_down):
    source = jnp.arange(SEQS, dtype=jnp.int32) // GROUP * GROUP + dealing.reshape(-1).astype(jnp.int32)
    holder = jnp.zeros((SEQS,), jnp.int32).at[source].set(jnp.arange(SEQS, dtype=jnp.int32))
    dealt_lengths = lengths[source]

    def forward(inputs_f, gain_a, mat_q, mat_k, mat_v, gain_q, gain_k, mat_o, gain_f, mat_g, mat_u, mat_d):
        params = (gain_a, low(mat_q), low(mat_k), low(mat_v), gain_q, gain_k, low(mat_o), gain_f, low(mat_g), low(mat_u), low(mat_d))
        dealt_rows = inputs_f[source]

        def one_slot(carried):
            return slot_layer(carried, params)
        results = lax.map(jax.checkpoint(one_slot), (dealt_rows, dealt_lengths, routes, gate_values))
        return results[holder]
    output, pullback = jax.vjp(forward, inputs.astype(jnp.float32), attn_gain, w_query, w_key, w_value, query_gain, key_gain, w_out, ffn_gain, w_gate, w_up, w_down)
    grads = pullback(cotangent.astype(jnp.float32))
    return (output.astype(jnp.bfloat16), grads[0].astype(jnp.bfloat16), grads[1], grads[2], grads[3], grads[4], grads[5], grads[6], grads[7], grads[8], grads[9], grads[10], grads[11])
```

```python
import math

import jax
import jax.numpy as jnp
from jax import lax
from jax.sharding import PartitionSpec as P

HEADS = 16


epsilon = 1e-05


def norm_scale(values):
    return lax.rsqrt(jnp.mean(values * values, axis=-1, keepdims=True) + epsilon)


def norm_back(normed, row_scale, incoming):
    return row_scale * (incoming - normed * jnp.mean(incoming * normed, axis=-1, keepdims=True))


def angle_tables(length_rows, head_size):
    half_size = head_size // 2
    position = jnp.arange(length_rows, dtype=jnp.float32)[:, None]
    inverse = jnp.exp(
        jnp.arange(half_size, dtype=jnp.float32) * (-2.0 * math.log(10000.0) / head_size)
    )
    angles = position * inverse[None, :]
    return (jnp.cos(angles)[:, None, :], jnp.sin(angles)[:, None, :])


def rotate_pairs(values, cosine, sine_table):
    half_size = values.shape[-1] // 2
    first = values[..., :half_size]
    second = values[..., half_size:]
    return jnp.concatenate(
        [first * cosine - second * sine_table, second * cosine + first * sine_table], axis=-1
    )


AXES = ("dp", "expert")


def expert_tables(routes, gates, expert, capacity):
    named = routes == expert
    member = jnp.any(named, axis=1)
    token_gate = jnp.sum(jnp.where(named, gates, 0.0), axis=1)
    tokens = member.shape[1]
    earlier = (
        jnp.arange(tokens, dtype=jnp.int32)[:, None] < jnp.arange(tokens, dtype=jnp.int32)[None, :]
    ).astype(jnp.float32)
    rank = jnp.dot(member.astype(jnp.float32), earlier, precision=lax.Precision.HIGHEST)
    place = jnp.where(member, rank.astype(jnp.int32), -1)
    hit = place[:, None, :] == jnp.arange(capacity, dtype=jnp.int32)[None, :, None]
    row_gate = jnp.sum(jnp.where(hit, token_gate[:, None, :], 0.0), axis=2)
    return hit, row_gate


def per_device(
    inputs,
    cotangent,
    lengths,
    dealing,
    routes,
    gate_values,
    attn_gain,
    w_query,
    w_key,
    w_value,
    query_gain,
    key_gain,
    w_out,
    ffn_gain,
    w_gate,
    w_up,
    w_down,
):
    low = jnp.bfloat16
    wide = jnp.float32
    group_size = lax.axis_size("expert")
    groups = lax.axis_size("dp")
    seqs = groups * group_size
    position = lax.axis_index("expert")
    group = lax.axis_index("dp")
    seq_inputs = inputs[0].astype(wide)
    seq_grads = cotangent[0].astype(wide)
    seq_length = lengths[position]
    length_rows, width = seq_inputs.shape
    head_size = width // HEADS
    top_count = routes.shape[2]
    local_experts, rows_held, hidden = w_gate.shape
    experts = local_experts * group_size
    capacity = length_rows * top_count * 9 // (8 * experts)
    shards = groups // local_experts
    expert = position * local_experts + group // shards
    block = hidden // groups
    hidden_part = hidden // shards

    payload = jnp.zeros((3 * top_count, length_rows), wide)
    payload = payload.at[:top_count].set(routes[0].T.astype(wide))
    payload = payload.at[top_count : 2 * top_count].set(gate_values[0].T)
    payload = payload.at[2 * top_count, :group_size].set(dealing[0].astype(wide))
    tables = lax.all_gather(payload, AXES, axis=0, tiled=False)
    deals = tables[:, 2 * top_count, :group_size].reshape(groups, group_size, group_size)[:, 0]
    deals = deals.astype(jnp.int32)
    slot_of = jnp.argmax(
        deals[:, None, :] == jnp.arange(group_size, dtype=jnp.int32)[None, :, None], axis=2
    )
    slot_of = (slot_of + jnp.arange(groups)[:, None] * group_size).reshape(-1)
    given = tables[slot_of]
    all_routes = given[:, :top_count].astype(jnp.int32)
    all_gates = given[:, top_count : 2 * top_count]
    hit, row_gate = expert_tables(all_routes, all_gates, expert, capacity)
    joined = 16 // math.gcd(16, capacity)
    bundles = seqs // joined
    eye = jnp.eye(joined, dtype=bool)
    select = (
        (hit.reshape(bundles, joined, capacity, 1, length_rows) & eye[None, :, None, :, None])
        .reshape(bundles, joined * capacity, joined * length_rows)
        .astype(low)
    )
    row_gate = row_gate.reshape(bundles, joined * capacity, 1)
    total_rows = seqs * capacity

    def to_owner(mat):
        mat = mat.astype(low).reshape(local_experts, rows_held, local_experts, shards, block)
        mat = mat.transpose(0, 3, 1, 2, 4).reshape(groups, rows_held, hidden_part)
        mat = lax.all_to_all(mat, "dp", split_axis=0, concat_axis=0, tiled=True)
        return mat.reshape(groups * rows_held, hidden_part)

    def to_master(grad):
        grad = grad.astype(low).reshape(groups, rows_held, hidden_part)
        grad = lax.all_to_all(grad, "dp", split_axis=0, concat_axis=0, tiled=True)
        grad = grad.reshape(local_experts, shards, rows_held, local_experts, block)
        return grad.transpose(0, 2, 3, 1, 4).reshape(local_experts, rows_held, hidden).astype(wide)

    same_shard = [
        [part + shards * index for index in range(local_experts)] for part in range(shards)
    ]

    def swap_down(mat):
        return lax.all_to_all(
            mat, "dp", split_axis=0, concat_axis=0, axis_index_groups=same_shard, tiled=True
        )

    gate_mat = to_owner(w_gate)
    up_mat = to_owner(w_up)
    down_mat = swap_down(w_down.astype(low)).reshape(hidden_part, width)

    attn_mats = (
        lax.all_gather(w_query.astype(low), AXES, axis=0, tiled=True),
        lax.all_gather(w_key.astype(low), AXES, axis=0, tiled=True),
        lax.all_gather(w_value.astype(low), AXES, axis=0, tiled=True),
        lax.all_gather(w_out.astype(low), AXES, axis=0, tiled=True),
    )
    query_mat, key_mat, value_mat, out_mat = attn_mats
    all_cotangent = lax.all_gather(cotangent, AXES, axis=0, tiled=True)
    scale_in = norm_scale(seq_inputs)
    normed_in = seq_inputs * scale_in
    hidden_in = (normed_in * attn_gain).astype(jnp.bfloat16)
    query_raw = jnp.dot(hidden_in, query_mat, preferred_element_type=jnp.float32)
    key_raw = jnp.dot(hidden_in, key_mat, preferred_element_type=jnp.float32)
    values = jnp.dot(hidden_in, value_mat, preferred_element_type=jnp.float32).astype(jnp.bfloat16)
    cosine, sine_table = angle_tables(length_rows, head_size)
    query_scale = norm_scale(query_raw)
    query_normed = query_raw * query_scale
    key_scale = norm_scale(key_raw)
    key_normed = key_raw * key_scale
    queries = rotate_pairs(
        (query_normed * query_gain).reshape(length_rows, HEADS, head_size), cosine, sine_table
    ).astype(jnp.bfloat16)
    key_rows = rotate_pairs(
        (key_normed * key_gain).reshape(length_rows, HEADS, head_size), cosine, sine_table
    ).astype(jnp.bfloat16)
    head_values = values.reshape(length_rows, HEADS, head_size)
    factor = head_size ** (-0.5)
    row_index = jnp.arange(length_rows, dtype=jnp.int32)[:, None]
    col_index = jnp.arange(length_rows, dtype=jnp.int32)[None, :]
    visible = (col_index <= row_index) & (col_index < seq_length)
    scores = (
        jnp.einsum("ihd,jhd->hij", queries, key_rows, preferred_element_type=jnp.float32) * factor
    )
    scores = jnp.where(visible[None], scores, -1e30)
    weights = jax.nn.softmax(scores, axis=-1)
    weights_low = weights.astype(jnp.bfloat16)
    attended = jnp.einsum(
        "hij,jhd->ihd", weights_low, head_values, preferred_element_type=jnp.float32
    )
    attended = attended.reshape(length_rows, width).astype(jnp.bfloat16)
    residual = seq_inputs + jnp.dot(attended, out_mat, preferred_element_type=jnp.float32)
    scale_mid = norm_scale(residual)
    normed_mid = residual * scale_mid
    hidden_mid = (normed_mid * ffn_gain).astype(jnp.bfloat16)
    all_hidden = lax.all_gather(hidden_mid[None], AXES, axis=0, tiled=True)
    bundled = all_hidden.reshape(bundles, joined * length_rows, width)
    rows = jnp.einsum("bct,btd->bcd", select, bundled, preferred_element_type=wide).astype(low)
    rows = rows.reshape(total_rows, width)
    bundled_grads = all_cotangent.reshape(bundles, joined * length_rows, width)
    out_grads = (
        row_gate
        * jnp.einsum("bct,btd->bcd", select, bundled_grads, preferred_element_type=wide)
    ).astype(low)
    out_grads = out_grads.reshape(total_rows, width)
    gate_pre = jnp.dot(rows, gate_mat, preferred_element_type=wide)
    up_pre = jnp.dot(rows, up_mat, preferred_element_type=wide)
    sigmoid_gate = jax.nn.sigmoid(gate_pre)
    hidden_act = (gate_pre * sigmoid_gate * up_pre).astype(low)
    expert_out = (
        row_gate
        * jnp.dot(hidden_act, down_mat, preferred_element_type=wide).reshape(
            bundles, joined * capacity, width
        )
    ).astype(low)
    out_part = jnp.einsum("bct,bcd->btd", select, expert_out, preferred_element_type=wide)
    out_part = out_part.astype(low).reshape(seqs, length_rows, width)
    grad_hidden = jnp.einsum("md,fd->mf", out_grads, down_mat, preferred_element_type=wide)
    grad_gate_pre = (
        grad_hidden * up_pre * sigmoid_gate * (1.0 + gate_pre * (1.0 - sigmoid_gate))
    ).astype(low)
    grad_up_pre = (grad_hidden * gate_pre * sigmoid_gate).astype(low)
    grad_slots = (
        jnp.einsum("mf,df->md", grad_gate_pre, gate_mat, preferred_element_type=wide)
        + jnp.einsum("mf,df->md", grad_up_pre, up_mat, preferred_element_type=wide)
    ).astype(low)
    mid_part = jnp.einsum(
        "bct,bcd->btd",
        select,
        grad_slots.reshape(bundles, joined * capacity, width),
        preferred_element_type=wide,
    )
    mid_part = mid_part.astype(low).reshape(seqs, length_rows, width)
    grad_mid = lax.psum_scatter(mid_part, AXES, scatter_dimension=0, tiled=True)[0].astype(wide)
    mixture = lax.psum_scatter(out_part, AXES, scatter_dimension=0, tiled=True)[0].astype(wide)
    layer_rows = (residual + mixture).astype(low)
    grad_down = jnp.einsum("mf,md->fd", hidden_act, out_grads, preferred_element_type=wide)
    grad_gate = jnp.einsum("md,mf->df", rows, grad_gate_pre, preferred_element_type=wide)
    grad_up = jnp.einsum("md,mf->df", rows, grad_up_pre, preferred_element_type=wide)
    expert_grads = (
        to_master(grad_gate),
        to_master(grad_up),
        swap_down(grad_down.astype(low).reshape(local_experts, block, width)).astype(wide),
    )
    ffn_gain_part = jnp.sum(grad_mid * normed_mid, axis=0)
    grad_resid = seq_grads + norm_back(normed_mid, scale_mid, grad_mid * ffn_gain)
    resid_low = grad_resid.astype(jnp.bfloat16)
    grad_out_mat = jnp.einsum("td,te->de", attended, resid_low, preferred_element_type=jnp.float32)
    grad_attended = jnp.einsum(
        "te,de->td", resid_low, out_mat, preferred_element_type=jnp.float32
    ).astype(jnp.bfloat16)
    grad_attended = grad_attended.reshape(length_rows, HEADS, head_size)
    grad_values = jnp.einsum(
        "hij,ihd->jhd", weights_low, grad_attended, preferred_element_type=jnp.float32
    )
    grad_values = grad_values.reshape(length_rows, width).astype(jnp.bfloat16)
    grad_weights = jnp.einsum(
        "ihd,jhd->hij", grad_attended, head_values, preferred_element_type=jnp.float32
    )
    grad_scores = (
        weights * (grad_weights - jnp.sum(weights * grad_weights, axis=-1, keepdims=True))
    ).astype(jnp.bfloat16)
    grad_queries = (
        jnp.einsum("hij,jhd->ihd", grad_scores, key_rows, preferred_element_type=jnp.float32)
        * factor
    )
    grad_keys = (
        jnp.einsum("hij,ihd->jhd", grad_scores, queries, preferred_element_type=jnp.float32)
        * factor
    )
    query_turned = rotate_pairs(grad_queries, cosine, -sine_table).reshape(length_rows, width)
    key_turned = rotate_pairs(grad_keys, cosine, -sine_table).reshape(length_rows, width)
    query_gain_part = jnp.sum(query_turned * query_normed, axis=0)
    key_gain_part = jnp.sum(key_turned * key_normed, axis=0)
    grad_query_raw = norm_back(query_normed, query_scale, query_turned * query_gain).astype(
        jnp.bfloat16
    )
    grad_key_raw = norm_back(key_normed, key_scale, key_turned * key_gain).astype(jnp.bfloat16)
    grad_query_mat = jnp.einsum(
        "td,te->de", hidden_in, grad_query_raw, preferred_element_type=jnp.float32
    )
    grad_key_mat = jnp.einsum(
        "td,te->de", hidden_in, grad_key_raw, preferred_element_type=jnp.float32
    )
    grad_value_mat = jnp.einsum(
        "td,te->de", hidden_in, grad_values, preferred_element_type=jnp.float32
    )
    grad_hidden_in = jnp.einsum(
        "te,de->td", grad_query_raw, query_mat, preferred_element_type=jnp.float32
    )
    grad_hidden_in = grad_hidden_in + jnp.einsum(
        "te,de->td", grad_key_raw, key_mat, preferred_element_type=jnp.float32
    )
    grad_hidden_in = grad_hidden_in + jnp.einsum(
        "te,de->td", grad_values, value_mat, preferred_element_type=jnp.float32
    )
    attn_gain_part = jnp.sum(grad_hidden_in * normed_in, axis=0)
    grad_seq = grad_resid + norm_back(normed_in, scale_in, grad_hidden_in * attn_gain)

    def to_rows(grad):
        return lax.psum_scatter(grad.astype(low), AXES, scatter_dimension=0, tiled=True).astype(wide)

    gain_parts = jnp.stack([attn_gain_part, query_gain_part, key_gain_part, ffn_gain_part])
    gains = lax.psum_scatter(gain_parts, AXES, scatter_dimension=1, tiled=True)
    return (
        layer_rows[None],
        grad_seq.astype(low)[None],
        gains[0],
        to_rows(grad_query_mat),
        to_rows(grad_key_mat),
        to_rows(grad_value_mat),
        gains[1],
        gains[2],
        to_rows(grad_out_mat),
        gains[3],
        *expert_grads,
    )


def solution(mesh):
    return jax.shard_map(
        per_device,
        mesh=mesh,
        in_specs=(
            P(("dp", "expert"), None, None),
            P(("dp", "expert"), None, None),
            P("dp"),
            P("dp", None),
            P(("dp", "expert"), None, None),
            P(("dp", "expert"), None, None),
            P(),
            P(("dp", "expert"), None),
            P(("dp", "expert"), None),
            P(("dp", "expert"), None),
            P(),
            P(),
            P(("dp", "expert"), None),
            P(),
            P("expert", "dp", None),
            P("expert", "dp", None),
            P("expert", "dp", None),
        ),
        out_specs=(
            P(("dp", "expert"), None, None),
            P(("dp", "expert"), None, None),
            P(("dp", "expert")),
            P(("dp", "expert"), None),
            P(("dp", "expert"), None),
            P(("dp", "expert"), None),
            P(("dp", "expert")),
            P(("dp", "expert")),
            P(("dp", "expert"), None),
            P(("dp", "expert")),
            P("expert", "dp", None),
            P("expert", "dp", None),
            P("expert", "dp", None),
        ),
        check_vma=False,
    )
```

```python
import functools
import math

import jax
import jax.numpy as jnp
from jax import lax
from jax.experimental import pallas as pl
from jax.experimental.pallas import tpu as pltpu
from jax.sharding import PartitionSpec as P

HEADS = 16


epsilon = 1e-05


def norm_scale(values):
    return lax.rsqrt(jnp.mean(values * values, axis=-1, keepdims=True) + epsilon)


def norm_back(normed, row_scale, incoming):
    return row_scale * (incoming - normed * jnp.mean(incoming * normed, axis=-1, keepdims=True))


def angle_tables(length_rows, head_size):
    half_size = head_size // 2
    position = jnp.arange(length_rows, dtype=jnp.float32)[:, None]
    inverse = jnp.exp(
        jnp.arange(half_size, dtype=jnp.float32) * (-2.0 * math.log(10000.0) / head_size)
    )
    angles = position * inverse[None, :]
    return (jnp.cos(angles)[:, None, :], jnp.sin(angles)[:, None, :])


def rotate_pairs(values, cosine, sine_table):
    half_size = values.shape[-1] // 2
    first = values[..., :half_size]
    second = values[..., half_size:]
    return jnp.concatenate(
        [first * cosine - second * sine_table, second * cosine + first * sine_table], axis=-1
    )


AXES = ("dp", "expert")
MESH = pl.DeviceIdType.MESH


def torus(groups, group_size):
    return 4, groups // 4, group_size // 2


def place(sizes):
    _, rows, columns = sizes
    dp, ep = lax.axis_index("dp"), lax.axis_index("expert")
    return dp // rows, lax.rem(dp, rows), ep // 2, lax.rem(ep, 2)


def shift(index, step, size):
    return lax.rem(index + step, size)


def greet(sizes, spot):
    na, nb, nc = sizes
    a, b, c, k = spot
    barrier = pltpu.get_barrier_semaphore()
    peers = [(shift(a, s, na), b, c, k) for s in range(1, na)]
    peers += [(a, shift(b, s, nb), c, k) for s in range(1, nb)]
    peers += [(a, b, shift(c, s, nc), k) for s in range(1, nc)]
    peers += [(a, b, c, 1 - k)]
    for peer in peers:
        pl.semaphore_signal(barrier, inc=1, device_id=address(sizes, peer), device_id_type=MESH)
    pl.semaphore_wait(barrier, len(peers))


def address(sizes, spot):
    a, b, c, k = spot
    return (a * sizes[1] + b, c * 2 + k)


def gather_kernel(sizes, arrays, jobs, *refs):
    na, nb, nc = sizes
    count = len(jobs)
    own_sem, send_sem, recv_sem, pair_send, pair_recv = refs[2 * arrays :]

    def held(chunk):
        array, start, rows = jobs[chunk]
        return refs[array].at[pl.ds(start, rows)]

    def landed(chunk, block):
        array, start, rows = jobs[chunk]
        return refs[arrays + array].at[index(*block), pl.ds(start, rows)]

    spot = place(sizes)
    a, b, c, k = spot

    def index(a, b, c, k):
        return (a * nb + b) * (2 * nc) + c * 2 + k

    greet(sizes, spot)
    sent = []

    def half(ref, part):
        if part is None:
            return ref
        rows = ref.shape[0] // 2
        return ref.at[pl.ds(part * rows, rows)]

    def slot(da, db, dc, part):
        base = (da * nb + db) * nc + dc
        return base if part is None or part == 0 else na * nb * nc + base

    def push(chunk, source, peer, block, da, db, dc, part):
        dst = landed(chunk, block)
        n = len(sent)
        copy = pltpu.make_async_remote_copy(
            src_ref=half(source, part), dst_ref=half(dst, part),
            send_sem=send_sem.at[n], recv_sem=recv_sem.at[chunk, slot(da, db, dc, part)],
            device_id=address(sizes, peer), device_id_type=MESH)
        copy.start()
        sent.append(copy)

    pairs = []

    def pair(chunk, source, block, da, db, dc, part):
        dst = landed(chunk, block)
        copy = pltpu.make_async_remote_copy(
            src_ref=half(source, part), dst_ref=half(dst, part),
            send_sem=pair_send.at[len(pairs)], recv_sem=pair_recv.at[chunk, slot(da, db, dc, part)],
            device_id=address(sizes, (a, b, c, 1 - k)), device_id_type=MESH)
        copy.start()
        pairs.append(copy)

    def arrived(chunk, da, db, dc, part):
        block = (shift(a, na - da, na), shift(b, nb - db, nb), shift(c, nc - dc, nc), k)
        ref = landed(chunk, block)
        view = half(ref, part)
        pltpu.make_async_copy(view, view, recv_sem.at[chunk, slot(da, db, dc, part)]).wait()
        return ref, block

    def line(chunk, source, block, da):
        for s in range(1, nb):
            push(chunk, source, (a, shift(b, s, nb), c, k), block, da, s, 0, None)
        for s in range(1, nc):
            push(chunk, source, (a, b, shift(c, s, nc), k), block, da, 0, s, None)
        pair(chunk, source, block, da, 0, 0, None)

    def first(chunk):
        block = (a, b, c, k)
        for s in range(1, na):
            push(chunk, held(chunk), (shift(a, s, na), b, c, k), block, s, 0, 0, None)
        line(chunk, held(chunk), block, 0)

    def second(chunk):
        for da in range(1, na):
            ref, block = arrived(chunk, da, 0, 0, None)
            line(chunk, ref, block, da)

    def third(chunk):
        for da in range(na):
            for db in range(1, nb):
                ref, block = arrived(chunk, da, db, 0, None)
                for s in range(1, nc):
                    push(chunk, ref, (a, b, shift(c, s, nc), k), block, da, db, s, 0)
                pair(chunk, ref, block, da, db, 0, None)
            for dc in range(1, nc):
                ref, block = arrived(chunk, da, 0, dc, None)
                for s in range(1, nb):
                    push(chunk, ref, (a, shift(b, s, nb), c, k), block, da, s, dc, 1)
                pair(chunk, ref, block, da, 0, dc, None)

    def fourth(chunk):
        for da in range(na):
            for db in range(1, nb):
                for dc in range(1, nc):
                    for part in (0, 1):
                        ref, block = arrived(chunk, da, db, dc, part)
                        pair(chunk, ref, block, da, db, dc, part)

    own = []
    for chunk in range(count):
        first(chunk)
        copy = pltpu.make_async_copy(
            held(chunk), landed(chunk, (a, b, c, k)), own_sem.at[chunk])
        copy.start()
        own.append(copy)
    for step in range(count + 2):
        if step < count:
            second(step)
        if 0 <= step - 1 < count:
            third(step - 1)
        if 0 <= step - 2 < count:
            fourth(step - 2)
    for chunk in range(count):
        own[chunk].wait()
        for da in range(na):
            for db in range(nb):
                for dc in range(nc):
                    for part in (0, 1) if db and dc else (None,):
                        block = (shift(a, na - da, na), shift(b, nb - db, nb), shift(c, nc - dc, nc), 1 - k)
                        view = half(landed(chunk, block), part)
                        pltpu.make_async_copy(
                            view, view, pair_recv.at[chunk, slot(da, db, dc, part)]).wait()
    for copy in sent:
        copy.wait_send()
    for copy in pairs:
        copy.wait_send()


def gather_all(blocks, pieces, collective_id):
    groups, group_size = lax.axis_size("dp"), lax.axis_size("expert")
    sizes = torus(groups, group_size)
    na, nb, nc = sizes
    arrays = len(blocks)
    total = na * nb * nc
    jobs = []
    for array, block in enumerate(blocks):
        cuts = max(1, min(pieces, block.shape[0] // 32, 128 // total))
        rows = block.shape[0] // cuts
        jobs += [(array, rows * cut, rows) for cut in range(cuts)]
    count = len(jobs)
    diag = na * (nb - 1) * (nc - 1)
    sends = count * (na - 1 + na * (nb - 1) + na * (nc - 1) + 2 * diag)
    pair_sends = count * (total + diag)
    dma = pltpu.SemaphoreType.DMA
    return pl.pallas_call(
        functools.partial(gather_kernel, sizes, arrays, tuple(jobs)),
        out_shape=[jax.ShapeDtypeStruct((groups * group_size,) + x.shape, x.dtype) for x in blocks],
        in_specs=[pl.BlockSpec(memory_space=pltpu.VMEM)] * arrays,
        out_specs=[pl.BlockSpec(memory_space=pl.ANY)] * arrays,
        scratch_shapes=[dma((count,)), dma((sends,)), dma((count, 2 * total)), dma((pair_sends,)),
                        dma((count, 2 * total))],
        compiler_params=pltpu.CompilerParams(collective_id=collective_id, has_side_effects=True),
    )(*blocks)


def loop(size, body):
    lax.fori_loop(0, size, lambda i, _: (body(i), None)[1], None)


def reduce_kernel(sizes, jobs, take, *refs):
    na, nb, nc = sizes
    plane = nb * nc
    total = na * plane
    count = len(jobs)
    (lhs, rhs, out, pair_out, held, diag_x, diag_y, from_x, from_y, from_z,
     pair_s, pair_r, dx_s, dx_r, dy_s, dy_r, x_s, x_r, y_s, y_r, z_s, z_r) = refs
    spot = place(sizes)
    a, b, c, k = spot
    rows = held.shape[2]
    part = rows // 2
    low, wide = held.dtype, jnp.float32
    greet(sizes, spot)

    def number(aa, bb, cc):
        return (aa * nb + bb) * nc + cc

    def mine(chunk, n, core):
        bb, cc = lax.rem(n // nc, nb), lax.rem(n, nc)
        block = (n // plane * nb + bb) * (2 * nc) + cc * 2 + core
        page, start = take(jobs[chunk], block)
        left_page, right_page = page if isinstance(page, tuple) else (page, page)
        left = lhs[left_page, pl.ds(pl.multiple_of(start, part), rows)]
        return jnp.dot(left, rhs[right_page], preferred_element_type=wide)

    def send(src, dst, s_sem, r_sem, peer):
        pltpu.make_async_remote_copy(
            src_ref=src, dst_ref=dst, send_sem=s_sem, recv_sem=r_sem,
            device_id=address(sizes, peer), device_id_type=MESH).start()

    def wait(view, sem):
        pltpu.make_async_copy(view, view, sem).wait()

    first, last = pl.ds(0, part), pl.ds(part, part)

    def stage_pair(chunk):
        slot = chunk % 2
        def one(aa):
            ref = pair_out.at[slot, pl.ds(aa * plane, plane)]
            if chunk >= 2:
                wait(ref, pair_s.at[slot, aa])
            def fill(m):
                n = aa * plane + m
                pair_out[slot, n] = mine(chunk, n, 1 - k).astype(low)
            loop(plane, fill)
            send(ref, held.at[chunk, pl.ds(aa * plane, plane)], pair_s.at[slot, aa], pair_r.at[chunk, aa],
                 (a, b, c, 1 - k))
        loop(na, one)

    def stage_diag(chunk):
        def one(aa):
            wait(held.at[chunk, pl.ds(aa * plane, plane)], pair_r.at[chunk, aa])
            def add(m):
                n = aa * plane + m
                held[chunk, n] = (held[chunk, n].astype(wide) + mine(chunk, n, k)).astype(low)
            loop(plane, add)
            for db in range(1, nb):
                bb = shift(b, db, nb)
                for dc in range(1, nc):
                    cc = shift(c, dc, nc)
                    m = (db - 1) * (nc - 1) + dc - 1
                    n = number(aa, bb, cc)
                    send(held.at[chunk, n, last], diag_x.at[chunk, m, aa], dx_s.at[chunk, m, aa],
                         dx_r.at[chunk, m, aa], (a, bb, c, k))
                    send(held.at[chunk, n, first], diag_y.at[chunk, m, aa], dy_s.at[chunk, m, aa],
                         dy_r.at[chunk, m, aa], (a, b, cc, k))
            for db in range(1, nb):
                bb = shift(b, db, nb)
                send(held.at[chunk, number(aa, bb, c), last], from_x.at[chunk, db - 1, aa, last],
                     x_s.at[chunk, db - 1, aa, 1], x_r.at[chunk, db - 1, aa, 1], (a, bb, c, k))
            for dc in range(1, nc):
                cc = shift(c, dc, nc)
                send(held.at[chunk, number(aa, b, cc), first], from_y.at[chunk, dc - 1, aa, first],
                     y_s.at[chunk, dc - 1, aa, 0], y_r.at[chunk, dc - 1, aa, 0], (a, b, cc, k))
        loop(na, one)

    def stage_turn(chunk):
        def one(aa):
            for db in range(1, nb):
                bb = shift(b, db, nb)
                n = number(aa, bb, c)
                value = held[chunk, n, first].astype(wide)
                for dc in range(1, nc):
                    m = (db - 1) * (nc - 1) + dc - 1
                    wait(diag_y.at[chunk, m, aa], dy_r.at[chunk, m, aa])
                    value += diag_y[chunk, m, aa].astype(wide)
                held[chunk, n, first] = value.astype(low)
                send(held.at[chunk, n, first], from_x.at[chunk, db - 1, aa, first],
                     x_s.at[chunk, db - 1, aa, 0], x_r.at[chunk, db - 1, aa, 0], (a, bb, c, k))
            for dc in range(1, nc):
                cc = shift(c, dc, nc)
                n = number(aa, b, cc)
                value = held[chunk, n, last].astype(wide)
                for db in range(1, nb):
                    m = (db - 1) * (nc - 1) + dc - 1
                    wait(diag_x.at[chunk, m, aa], dx_r.at[chunk, m, aa])
                    value += diag_x[chunk, m, aa].astype(wide)
                held[chunk, n, last] = value.astype(low)
                send(held.at[chunk, n, last], from_y.at[chunk, dc - 1, aa, last],
                     y_s.at[chunk, dc - 1, aa, 1], y_r.at[chunk, dc - 1, aa, 1], (a, b, cc, k))
        loop(na, one)

    def stage_line(chunk):
        def one(da):
            aa = shift(a, da + 1, na)
            n = number(aa, b, c)
            value = held[chunk, n].astype(wide)
            for db in range(nb - 1):
                for side, where in ((1, last), (0, first)):
                    wait(from_x.at[chunk, db, aa, where], x_r.at[chunk, db, aa, side])
                value += from_x[chunk, db, aa].astype(wide)
            for dc in range(nc - 1):
                for side, where in ((0, first), (1, last)):
                    wait(from_y.at[chunk, dc, aa, where], y_r.at[chunk, dc, aa, side])
                value += from_y[chunk, dc, aa].astype(wide)
            held[chunk, n] = value.astype(low)
            @pl.when(da < na - 1)
            def _():
                send(held.at[chunk, n], from_z.at[chunk, da], z_s.at[chunk, da], z_r.at[chunk, da], (aa, b, c, k))
        loop(na, one)

    def stage_end(chunk):
        value = held[chunk, number(a, b, c)].astype(wide)
        for da in range(na - 1):
            wait(from_z.at[chunk, da], z_r.at[chunk, da])
            value += from_z[chunk, da].astype(wide)
        out[chunk] = value.astype(out.dtype)

    stages = (stage_pair, stage_diag, stage_turn, stage_line, stage_end)
    lags = (0, 1, 2, 3, 4)
    for step in range(count + lags[-1]):
        for stage, lag in zip(stages, lags):
            if 0 <= step - lag < count:
                stage(step - lag)

    for chunk in range(count):
        def one(aa):
            if chunk >= count - 2:
                wait(pair_out.at[chunk % 2, pl.ds(aa * plane, plane)], pair_s.at[chunk % 2, aa])
            for m in range((nb - 1) * (nc - 1)):
                wait(diag_x.at[chunk, m, aa], dx_s.at[chunk, m, aa])
                wait(diag_y.at[chunk, m, aa], dy_s.at[chunk, m, aa])
            for db in range(nb - 1):
                wait(from_x.at[chunk, db, aa, first], x_s.at[chunk, db, aa, 0])
                wait(from_x.at[chunk, db, aa, last], x_s.at[chunk, db, aa, 1])
            for dc in range(nc - 1):
                wait(from_y.at[chunk, dc, aa, first], y_s.at[chunk, dc, aa, 0])
                wait(from_y.at[chunk, dc, aa, last], y_s.at[chunk, dc, aa, 1])
        loop(na, one)
        def two(da):
            wait(from_z.at[chunk, da], z_s.at[chunk, da])
        loop(na - 1, two)


def reduce_call(lhs, rhs, jobs, take, rows, collective_id):
    groups, group_size = lax.axis_size("dp"), lax.axis_size("expert")
    sizes = torus(groups, group_size)
    na, nb, nc = sizes
    total = na * nb * nc
    width = rhs.shape[-1]
    count = len(jobs)
    low = jnp.bfloat16
    diag = (nb - 1) * (nc - 1)
    dma = pltpu.SemaphoreType.DMA
    both = lambda *shape: [dma(shape), dma(shape)]
    return pl.pallas_call(
        functools.partial(reduce_kernel, sizes, jobs, take),
        out_shape=jax.ShapeDtypeStruct((count, rows, width), jnp.float32),
        in_specs=[pl.BlockSpec(memory_space=pltpu.VMEM)] * 2,
        out_specs=pl.BlockSpec(memory_space=pltpu.VMEM),
        scratch_shapes=[
            pltpu.VMEM((2, total, rows, width), low),
            pltpu.VMEM((count, total, rows, width), low),
            pltpu.VMEM((count, diag, na, rows // 2, width), low),
            pltpu.VMEM((count, diag, na, rows // 2, width), low),
            pltpu.VMEM((count, nb - 1, na, rows, width), low),
            pltpu.VMEM((count, nc - 1, na, rows, width), low),
            pltpu.VMEM((count, na - 1, rows, width), low),
            dma((2, na)), dma((count, na)),
            *both(count, diag, na), *both(count, diag, na),
            *both(count, nb - 1, na, 2), *both(count, nc - 1, na, 2),
            *both(count, na - 1),
        ],
        compiler_params=pltpu.CompilerParams(collective_id=collective_id, has_side_effects=True,
                                             vmem_limit_bytes=64_000_000),
    )(lhs, rhs)


def padded(array):
    return math.prod(array.shape[:-1]) * (-(-array.shape[-1] // 128) * 128) * array.dtype.itemsize


def reduce_all(lhs, rhs, jobs, take, rows, collective_id):
    groups, group_size = lax.axis_size("dp"), lax.axis_size("expert")
    na, nb, nc = torus(groups, group_size)
    total = na * nb * nc
    line = rows * rhs.shape[-1] * 2
    diag = (nb - 1) * (nc - 1)
    each = line * (total + diag * na + (nb - 1 + nc - 1) * na + na - 1) + 2 * line
    spare = 58_000_000 - padded(lhs) - padded(rhs) - 2 * total * line
    fit = max(1, spare // each)
    calls = -(-len(jobs) // fit)
    size = -(-len(jobs) // calls)
    parts = [
        reduce_call(lhs, rhs, tuple(jobs[at : at + size]), take, rows, collective_id + at)
        for at in range(0, len(jobs), size)
    ]
    return parts[0] if len(parts) == 1 else jnp.concatenate(parts, axis=0)


def expert_tables(routes, gates, expert, capacity):
    named = routes == expert
    member = jnp.any(named, axis=1)
    token_gate = jnp.sum(jnp.where(named, gates, 0.0), axis=1)
    tokens = member.shape[1]
    earlier = (
        jnp.arange(tokens, dtype=jnp.int32)[:, None] < jnp.arange(tokens, dtype=jnp.int32)[None, :]
    ).astype(jnp.float32)
    rank = jnp.dot(member.astype(jnp.float32), earlier, precision=lax.Precision.HIGHEST)
    place = jnp.where(member, rank.astype(jnp.int32), -1)
    hit = place[:, None, :] == jnp.arange(capacity, dtype=jnp.int32)[None, :, None]
    row_gate = jnp.sum(jnp.where(hit, token_gate[:, None, :], 0.0), axis=2)
    return hit, row_gate


def per_device(
    inputs,
    cotangent,
    lengths,
    dealing,
    routes,
    gate_values,
    attn_gain,
    w_query,
    w_key,
    w_value,
    query_gain,
    key_gain,
    w_out,
    ffn_gain,
    w_gate,
    w_up,
    w_down,
):
    low = jnp.bfloat16
    wide = jnp.float32
    group_size = lax.axis_size("expert")
    groups = lax.axis_size("dp")
    seqs = groups * group_size
    position = lax.axis_index("expert")
    group = lax.axis_index("dp")
    seq_inputs = inputs[0].astype(wide)
    seq_grads = cotangent[0].astype(wide)
    seq_length = lengths[position]
    length_rows, width = seq_inputs.shape
    head_size = width // HEADS
    top_count = routes.shape[2]
    local_experts, rows_held, hidden = w_gate.shape
    experts = local_experts * group_size
    capacity = length_rows * top_count * 9 // (8 * experts)
    shards = groups // local_experts
    expert = position * local_experts + group // shards
    block = hidden // groups
    hidden_part = hidden // shards

    payload = jnp.zeros((3 * top_count, length_rows), wide)
    payload = payload.at[:top_count].set(routes[0].T.astype(wide))
    payload = payload.at[top_count : 2 * top_count].set(gate_values[0].T)
    payload = payload.at[2 * top_count, :group_size].set(dealing[0].astype(wide))
    tables = lax.all_gather(payload, AXES, axis=0, tiled=False)
    deals = tables[:, 2 * top_count, :group_size].reshape(groups, group_size, group_size)[:, 0]
    deals = deals.astype(jnp.int32)
    slot_of = jnp.argmax(
        deals[:, None, :] == jnp.arange(group_size, dtype=jnp.int32)[None, :, None], axis=2
    )
    slot_of = (slot_of + jnp.arange(groups)[:, None] * group_size).reshape(-1)
    given = tables[slot_of]
    all_routes = given[:, :top_count].astype(jnp.int32)
    all_gates = given[:, top_count : 2 * top_count]
    hit, row_gate = expert_tables(all_routes, all_gates, expert, capacity)
    joined = 16 // math.gcd(16, capacity)
    bundles = seqs // joined
    eye = jnp.eye(joined, dtype=bool)
    select = (
        (hit.reshape(bundles, joined, capacity, 1, length_rows) & eye[None, :, None, :, None])
        .reshape(bundles, joined * capacity, joined * length_rows)
        .astype(low)
    )
    row_gate = row_gate.reshape(bundles, joined * capacity, 1)
    total_rows = seqs * capacity

    def to_owner(mat):
        mat = mat.astype(low).reshape(local_experts, rows_held, local_experts, shards, block)
        mat = mat.transpose(0, 3, 1, 2, 4).reshape(groups, rows_held, hidden_part)
        mat = lax.all_to_all(mat, "dp", split_axis=0, concat_axis=0, tiled=True)
        return mat.reshape(groups * rows_held, hidden_part)

    def to_master(grad):
        grad = grad.astype(low).reshape(groups, rows_held, hidden_part)
        grad = lax.all_to_all(grad, "dp", split_axis=0, concat_axis=0, tiled=True)
        grad = grad.reshape(local_experts, shards, rows_held, local_experts, block)
        return grad.transpose(0, 2, 3, 1, 4).reshape(local_experts, rows_held, hidden).astype(wide)

    same_shard = [
        [part + shards * index for index in range(local_experts)] for part in range(shards)
    ]

    def swap_down(mat):
        return lax.all_to_all(
            mat, "dp", split_axis=0, concat_axis=0, axis_index_groups=same_shard, tiled=True
        )

    gate_mat = to_owner(w_gate)
    up_mat = to_owner(w_up)
    down_mat = swap_down(w_down.astype(low)).reshape(hidden_part, width)

    attn_mats = gather_all(
        [w_query.astype(low), w_key.astype(low), w_value.astype(low), w_out.astype(low)], 2, 1
    )
    attn_mats = [mat.reshape(width, width) for mat in attn_mats]
    query_mat, key_mat, value_mat, out_mat = attn_mats
    all_cotangent = lax.all_gather(cotangent, AXES, axis=0, tiled=True)
    scale_in = norm_scale(seq_inputs)
    normed_in = seq_inputs * scale_in
    hidden_in = (normed_in * attn_gain).astype(jnp.bfloat16)
    query_raw = jnp.dot(hidden_in, query_mat, preferred_element_type=jnp.float32)
    key_raw = jnp.dot(hidden_in, key_mat, preferred_element_type=jnp.float32)
    values = jnp.dot(hidden_in, value_mat, preferred_element_type=jnp.float32).astype(jnp.bfloat16)
    cosine, sine_table = angle_tables(length_rows, head_size)
    query_scale = norm_scale(query_raw)
    query_normed = query_raw * query_scale
    key_scale = norm_scale(key_raw)
    key_normed = key_raw * key_scale
    queries = rotate_pairs(
        (query_normed * query_gain).reshape(length_rows, HEADS, head_size), cosine, sine_table
    ).astype(jnp.bfloat16)
    key_rows = rotate_pairs(
        (key_normed * key_gain).reshape(length_rows, HEADS, head_size), cosine, sine_table
    ).astype(jnp.bfloat16)
    head_values = values.reshape(length_rows, HEADS, head_size)
    factor = head_size ** (-0.5)
    row_index = jnp.arange(length_rows, dtype=jnp.int32)[:, None]
    col_index = jnp.arange(length_rows, dtype=jnp.int32)[None, :]
    visible = (col_index <= row_index) & (col_index < seq_length)
    scores = (
        jnp.einsum("ihd,jhd->hij", queries, key_rows, preferred_element_type=jnp.float32) * factor
    )
    scores = jnp.where(visible[None], scores, -1e30)
    weights = jax.nn.softmax(scores, axis=-1)
    weights_low = weights.astype(jnp.bfloat16)
    attended = jnp.einsum(
        "hij,jhd->ihd", weights_low, head_values, preferred_element_type=jnp.float32
    )
    attended = attended.reshape(length_rows, width).astype(jnp.bfloat16)
    residual = seq_inputs + jnp.dot(attended, out_mat, preferred_element_type=jnp.float32)
    scale_mid = norm_scale(residual)
    normed_mid = residual * scale_mid
    hidden_mid = (normed_mid * ffn_gain).astype(jnp.bfloat16)
    (all_hidden,) = gather_all([hidden_mid], 4, 2)
    bundled = all_hidden.reshape(bundles, joined * length_rows, width)
    rows = jnp.einsum("bct,btd->bcd", select, bundled, preferred_element_type=wide).astype(low)
    rows = rows.reshape(total_rows, width)
    bundled_grads = all_cotangent.reshape(bundles, joined * length_rows, width)
    out_grads = (
        row_gate
        * jnp.einsum("bct,btd->bcd", select, bundled_grads, preferred_element_type=wide)
    ).astype(low)
    out_grads = out_grads.reshape(total_rows, width)
    gate_pre = jnp.dot(rows, gate_mat, preferred_element_type=wide)
    up_pre = jnp.dot(rows, up_mat, preferred_element_type=wide)
    sigmoid_gate = jax.nn.sigmoid(gate_pre)
    hidden_act = (gate_pre * sigmoid_gate * up_pre).astype(low)
    expert_out = (
        row_gate
        * jnp.dot(hidden_act, down_mat, preferred_element_type=wide).reshape(
            bundles, joined * capacity, width
        )
    ).astype(low)
    grad_hidden = jnp.einsum("md,fd->mf", out_grads, down_mat, preferred_element_type=wide)
    grad_gate_pre = (
        grad_hidden * up_pre * sigmoid_gate * (1.0 + gate_pre * (1.0 - sigmoid_gate))
    ).astype(low)
    grad_up_pre = (grad_hidden * gate_pre * sigmoid_gate).astype(low)
    grad_slots = (
        jnp.einsum("mf,df->md", grad_gate_pre, gate_mat, preferred_element_type=wide)
        + jnp.einsum("mf,df->md", grad_up_pre, up_mat, preferred_element_type=wide)
    ).astype(low)
    placed = select.transpose(0, 2, 1)
    cuts = max(1, min(4, 128 // (seqs // 2)))
    cut_rows = length_rows // cuts if seqs <= 32 else 16
    token_jobs = [(0, start) for start in range(0, length_rows, cut_rows)]

    def token_take(job, block):
        return block // joined, lax.rem(block, joined) * length_rows + job[1]

    grad_mid = reduce_all(
        placed,
        grad_slots.reshape(bundles, joined * capacity, width),
        token_jobs,
        token_take,
        cut_rows,
        10,
    ).reshape(length_rows, width)
    mixture = reduce_all(placed, expert_out, token_jobs, token_take, cut_rows, 30)
    mixture = mixture.reshape(length_rows, width)
    layer_rows = (residual + mixture).astype(low)
    grad_down = jnp.einsum("mf,md->fd", hidden_act, out_grads, preferred_element_type=wide)
    grad_gate = jnp.einsum("md,mf->df", rows, grad_gate_pre, preferred_element_type=wide)
    grad_up = jnp.einsum("md,mf->df", rows, grad_up_pre, preferred_element_type=wide)
    expert_grads = (
        to_master(grad_gate),
        to_master(grad_up),
        swap_down(grad_down.astype(low).reshape(local_experts, block, width)).astype(wide),
    )
    ffn_gain_part = jnp.sum(grad_mid * normed_mid, axis=0)
    grad_resid = seq_grads + norm_back(normed_mid, scale_mid, grad_mid * ffn_gain)
    resid_low = grad_resid.astype(jnp.bfloat16)
    grad_attended = jnp.einsum(
        "te,de->td", resid_low, out_mat, preferred_element_type=jnp.float32
    ).astype(jnp.bfloat16)
    grad_attended = grad_attended.reshape(length_rows, HEADS, head_size)
    grad_values = jnp.einsum(
        "hij,ihd->jhd", weights_low, grad_attended, preferred_element_type=jnp.float32
    )
    grad_values = grad_values.reshape(length_rows, width).astype(jnp.bfloat16)
    grad_weights = jnp.einsum(
        "ihd,jhd->hij", grad_attended, head_values, preferred_element_type=jnp.float32
    )
    grad_scores = (
        weights * (grad_weights - jnp.sum(weights * grad_weights, axis=-1, keepdims=True))
    ).astype(jnp.bfloat16)
    grad_queries = (
        jnp.einsum("hij,jhd->ihd", grad_scores, key_rows, preferred_element_type=jnp.float32)
        * factor
    )
    grad_keys = (
        jnp.einsum("hij,ihd->jhd", grad_scores, queries, preferred_element_type=jnp.float32)
        * factor
    )
    query_turned = rotate_pairs(grad_queries, cosine, -sine_table).reshape(length_rows, width)
    key_turned = rotate_pairs(grad_keys, cosine, -sine_table).reshape(length_rows, width)
    query_gain_part = jnp.sum(query_turned * query_normed, axis=0)
    key_gain_part = jnp.sum(key_turned * key_normed, axis=0)
    grad_query_raw = norm_back(query_normed, query_scale, query_turned * query_gain).astype(
        jnp.bfloat16
    )
    grad_key_raw = norm_back(key_normed, key_scale, key_turned * key_gain).astype(jnp.bfloat16)
    grad_hidden_in = jnp.einsum(
        "te,de->td", grad_query_raw, query_mat, preferred_element_type=jnp.float32
    )
    grad_hidden_in = grad_hidden_in + jnp.einsum(
        "te,de->td", grad_key_raw, key_mat, preferred_element_type=jnp.float32
    )
    grad_hidden_in = grad_hidden_in + jnp.einsum(
        "te,de->td", grad_values, value_mat, preferred_element_type=jnp.float32
    )
    attn_gain_part = jnp.sum(grad_hidden_in * normed_in, axis=0)
    grad_seq = grad_resid + norm_back(normed_in, scale_in, grad_hidden_in * attn_gain)

    lhs = jnp.stack([hidden_in.T, attended.T])
    rhs = jnp.stack([grad_query_raw, grad_key_raw, grad_values, resid_low])
    held_rows = w_query.shape[0]
    weight_cuts = max(1, min(2, held_rows // 32))
    weight_rows = held_rows // weight_cuts
    weight_jobs = [
        (mat, cut * weight_rows) for mat in (3, 2, 1, 0) for cut in range(weight_cuts)
    ]

    def weight_take(job, block):
        return (1 if job[0] == 3 else 0, job[0]), block * held_rows + job[1]

    weight_grads = reduce_all(lhs, rhs, weight_jobs, weight_take, weight_rows, 50)
    weight_grads = weight_grads.reshape(4, held_rows, width)
    gain_parts = jnp.stack([attn_gain_part, query_gain_part, key_gain_part, ffn_gain_part])
    gains = lax.psum_scatter(gain_parts, AXES, scatter_dimension=1, tiled=True)
    return (
        layer_rows[None],
        grad_seq.astype(low)[None],
        gains[0],
        weight_grads[3],
        weight_grads[2],
        weight_grads[1],
        gains[1],
        gains[2],
        weight_grads[0],
        gains[3],
        *expert_grads,
    )


def solution(mesh):
    return jax.shard_map(
        per_device,
        mesh=mesh,
        in_specs=(
            P(("dp", "expert"), None, None),
            P(("dp", "expert"), None, None),
            P("dp"),
            P("dp", None),
            P(("dp", "expert"), None, None),
            P(("dp", "expert"), None, None),
            P(),
            P(("dp", "expert"), None),
            P(("dp", "expert"), None),
            P(("dp", "expert"), None),
            P(),
            P(),
            P(("dp", "expert"), None),
            P(),
            P("expert", "dp", None),
            P("expert", "dp", None),
            P("expert", "dp", None),
        ),
        out_specs=(
            P(("dp", "expert"), None, None),
            P(("dp", "expert"), None, None),
            P(("dp", "expert")),
            P(("dp", "expert"), None),
            P(("dp", "expert"), None),
            P(("dp", "expert"), None),
            P(("dp", "expert")),
            P(("dp", "expert")),
            P(("dp", "expert"), None),
            P(("dp", "expert")),
            P("expert", "dp", None),
            P("expert", "dp", None),
            P("expert", "dp", None),
        ),
        check_vma=False,
    )
```
